512 devices in a mesh: section: 16 (over y_hi, x, core), seq: 32 (over y_lo, z).
Axes of the slice: x: 4, y: 8 (y_hi: 2, y_lo: 4; y = y_hi * 4 + y_lo), z: 8, core: 2. Of those that a mesh axis runs over, the one named last changes fastest.
Arguments:
- hidden: bfloat16 [16, 512, 4096], P('section', 'seq'), may hold values from -6 to 6
- modulation: float32 [16, 3, 4096], P('section'), may hold values from -3 to 3
- w_qkv: bfloat16 [16, 4096, 3, 4096], P('section', None, None, 'seq'), may hold values from -0.09375 to 0.09375
- qk_gain: float32 [16, 2, 128], P('section'), may hold values from 1 to 2.5
- w_out: bfloat16 [16, 4096, 4096], P('section', 'seq'), may hold values from -0.1875 to 0.1875
- stale_kv: bfloat16 [16, 2, 1024, 4096], P('section', None, None, 'seq')
- patch_start: int32 [16], P('section'), may hold values from 0 to 512
Outputs:
- passed: bfloat16 [16, 512, 4096], P('section', 'seq')
The draws below stay inside these ranges and needn't reach their ends.
All inputs are finite; a program needn't handle non-finite values.
Results may differ from the reference program's by a relative error of at most 0.024.
Values may be sent and summed in bfloat16 or wider, within the bound.
A program may use at most 64 MiB of HBM per device.

```python
import math
import jax
import jax.numpy as jnp
from jax import lax

D = 4096
HD = 128
SECTIONS = 16
HEADS = 32
INNER = 4096
PATCH = 512
CLIP = 1024


def draw_stale_kv(key, part):
    base_key = jax.random.fold_in(jax.random.fold_in(key, 7), 0)
    base = jax.random.normal(base_key, (SECTIONS, 2, CLIP, INNER), jnp.float32)
    return base.astype(jnp.bfloat16)


def with_ends(values, key, least, largest):
    spot = [jax.random.randint(jax.random.fold_in(key, axis), (), 0, length) for axis, length in enumerate(values.shape)]
    main_axis = values.shape.index(max(values.shape))
    next_to = spot[:main_axis] + [(spot[main_axis] + 1) % values.shape[main_axis]] + spot[main_axis + 1:]
    return values.at[tuple(spot)].set(least).at[tuple(next_to)].set(largest)


def block_levels(stream_key, shape, shards, smallest, top_value):
    level, own = 1.0, jax.random.fold_in(stream_key, 6)
    for axis_at, shards_of in shards:
        heights = jnp.exp(jax.random.uniform(jax.random.fold_in(own, axis_at), (shards_of,), jnp.float32, smallest / len(shards), top_value / len(shards)))
        level = level * jnp.repeat(heights, shape[axis_at] // shards_of).reshape([-1 if axis == axis_at else 1 for axis in range(len(shape))])
    return level


def noise(stream_key, extent, deviation, bound, cuts=(), held_as=jnp.bfloat16):
    factor_of = block_levels(stream_key, extent, cuts, -0.22, 0.18) if cuts else 1.0
    values = jax.random.normal(stream_key, extent, jnp.float32) * deviation * factor_of
    return jnp.minimum(jnp.maximum(values, -bound), bound).astype(held_as)


def setup_inputs(seed: int = 0) -> dict:
    key_of = jax.random.split(jax.random.key(seed), 8)
    return {
        "hidden": noise(key_of[0], (SECTIONS, PATCH, D), 1.0, 6.0, ((0, 16), (1, 32))),
        "modulation": noise(key_of[1], (SECTIONS, 3, D), 0.6, 3.0, ((0, 16),), jnp.float32),
        "w_qkv": noise(key_of[2], (SECTIONS, D, 3, INNER), D ** -0.5, 0.09375, ((0, 16), (3, 32))),
        "qk_gain": jnp.clip(jnp.exp(math.log(2.5) - 0.916290732 * jax.random.uniform(key_of[3], (SECTIONS, 2, HD), jnp.float32) ** block_levels(key_of[3], (SECTIONS, 2, HD), ((0, 16),), -0.2, 0.2)), 1.0, 2.5),
        "w_out": noise(key_of[4], (SECTIONS, INNER, D), (INNER // 4) ** -0.5, 0.1875, ((0, 16), (1, 32))),
        "stale_kv": draw_stale_kv(jax.random.fold_in(key_of[7], 71), 0),
        "patch_start": with_ends(jax.random.randint(key_of[6], (SECTIONS,), 0, CLIP - PATCH + 1), jax.random.fold_in(key_of[6], 1), 0, CLIP - PATCH).astype(jnp.int32),
    }


def modulate(tokens_in, modulation):
    values = tokens_in.astype(jnp.float32)
    average = lax.optimization_barrier(jnp.mean(values, axis=-1, keepdims=True))
    centred = values - average
    spread = lax.optimization_barrier(jnp.mean(centred * centred, axis=-1, keepdims=True))
    normed = centred * lax.rsqrt(spread + 1e-06)
    return (values, (normed * (1.0 + modulation[1]) + modulation[0]).astype(jnp.bfloat16))

def head_norm(values, gains):
    return values * lax.rsqrt(lax.optimization_barrier(jnp.mean(values * values, axis=-1, keepdims=True)) + 1e-06) * gains

def attend(queries, keys_all, values_all):
    scores = jnp.dot(queries, keys_all.T, preferred_element_type=jnp.float32) / math.sqrt(HD)
    highest = lax.optimization_barrier(jnp.max(scores, axis=-1, keepdims=True))
    raised = jnp.exp(scores - highest)
    probs = (raised / lax.optimization_barrier(jnp.sum(raised, axis=-1, keepdims=True))).astype(jnp.bfloat16)
    return jnp.dot(probs, values_all, preferred_element_type=jnp.float32).astype(jnp.bfloat16)

def one_layer(tokens_in, modulation, w_qkv, qk_gain, w_out, stale_kv, patch_start):
    values, mixed = modulate(tokens_in, modulation)
    count = tokens_in.shape[0]
    merged = jnp.dot(mixed, w_qkv.reshape(D, 3 * INNER), preferred_element_type=jnp.float32)
    merged = merged.reshape(count, 3, HEADS, HD)
    queries = head_norm(merged[:, 0], qk_gain[0]).astype(jnp.bfloat16)
    keys_new = head_norm(merged[:, 1], qk_gain[1]).astype(jnp.bfloat16)
    values_new = merged[:, 2].astype(jnp.bfloat16)
    anchor = patch_start.astype(jnp.int32)
    nought = jnp.zeros((), jnp.int32)
    keys_all = lax.dynamic_update_slice(stale_kv[0].reshape(CLIP, HEADS, HD), keys_new, (anchor, nought, nought))
    values_all = lax.dynamic_update_slice(stale_kv[1].reshape(CLIP, HEADS, HD), values_new, (anchor, nought, nought))
    out_heads = w_out.reshape(HEADS, HD, D)

    def per_head(running, items):
        query_h, key_h, value_h, weight_h = items
        attended = attend(query_h, key_h, value_h)
        partial_value = jnp.dot(attended, weight_h, preferred_element_type=jnp.float32).astype(jnp.bfloat16)
        partial_value = lax.optimization_barrier(partial_value)
        return (running + partial_value.astype(jnp.float32), None)
    running, unused = lax.scan(per_head, jnp.zeros((count, D), jnp.float32), (queries.transpose(1, 0, 2), keys_all.transpose(1, 0, 2), values_all.transpose(1, 0, 2), out_heads))
    return (values + modulation[2] * running).astype(jnp.bfloat16)

def reference(hidden, modulation, w_qkv, qk_gain, w_out, stale_kv, patch_start):
    layers = lax.map(lambda items: one_layer(*items), (hidden, modulation, w_qkv, qk_gain, w_out, stale_kv, patch_start))
    return jnp.roll(layers, 1, axis=0)
```

```python
import functools
import math

import jax
import jax.numpy as jnp
from jax import lax
from jax.experimental import pallas as pl
from jax.experimental.pallas import tpu as pltpu
from jax.sharding import PartitionSpec as P

MESH = pl.DeviceIdType.MESH
NY = 4
NZ = 8
PEERS = (1, 3, 2)
ORDER = (4, 3, -3, 2, -2, 1, -1, 0)


def kernel(
    sections,
    hid,
    mod,
    wq_hbm,
    gain,
    wo_hbm,
    st_hbm,
    start,
    out,
    rows_all,
    w_all,
    w_cols,
    stale,
    keys,
    vals,
    queries,
    heads,
    part_out,
    part_in,
    hid_cols,
    out_rows,
    local_sem,
    y_send,
    y_recv,
    hid_send,
    hid_recv,
    w_send,
    w_recv,
    z_send,
    z_recv,
    head_send,
    head_recv,
    ring_send,
    ring_recv,
    out_send,
    out_recv,
):
    own, width = hid.shape
    head_size = gain.shape[1]
    block = NY * own
    half = block // 2
    cols = width // NY
    patch = block * NZ
    section = lax.axis_index("section")
    place = lax.axis_index("seq")
    y = place // NZ
    z = place % NZ
    after = (section + 1) % sections
    before = (section + sections - 1) % sections

    def y_at(distance):
        return (y + distance + NY) % NY

    def z_at(distance):
        return (z + distance + NZ) % NZ

    def remote(src, dst, send, recv, yy, zz, sec=section):
        return pltpu.make_async_remote_copy(
            src_ref=src,
            dst_ref=dst,
            send_sem=send,
            recv_sem=recv,
            device_id=(sec, yy * NZ + zz),
            device_id_type=MESH,
        )

    local = [
        pltpu.make_async_copy(
            wq_hbm.at[j], w_all.at[:, pl.ds(j * head_size, head_size)], local_sem.at[j]
        )
        for j in range(3)
    ]
    local.append(pltpu.make_async_copy(st_hbm, stale, local_sem.at[3]))
    my_cols = pl.ds(pl.multiple_of(y * cols, cols), cols)
    local.append(
        pltpu.make_async_copy(wo_hbm.at[:, my_cols], w_cols.at[y], local_sem.at[4])
    )
    for copy in local:
        copy.start()

    barrier = pltpu.get_barrier_semaphore()
    partners = [(section, y_at(e) * NZ + z) for e in PEERS]
    partners += [(section, y * NZ + z_at(s)) for s in (1, -1)]
    partners += [(after, yy * NZ + z) for yy in range(NY)]
    partners += [(before, yy * NZ + z) for yy in range(NY)]
    for partner in partners:
        pl.semaphore_signal(barrier, inc=1, device_id=partner, device_id_type=MESH)

    values = hid[...].astype(jnp.float32)
    average = jnp.mean(values, axis=-1, keepdims=True)
    centred = values - average
    spread = jnp.mean(centred * centred, axis=-1, keepdims=True)
    normed = centred * lax.rsqrt(spread + 1e-06)
    mixed = normed * (1.0 + mod[1:2, :]) + mod[0:1, :]
    rows_all[z, y] = mixed.astype(jnp.bfloat16)
    hid_cols[y] = hid[:, my_cols]

    pl.semaphore_wait(barrier, len(partners))

    def y_copy(e):
        mine = rows_all.at[z, y]
        return remote(mine, mine, y_send.at[e], y_recv.at[e], y_at(e), z)

    def y_wait(e):
        slot = rows_all.at[z, y_at(-e)]
        remote(slot, slot, y_send.at[e], y_recv.at[e], y_at(e), z).wait_recv()

    def z_copy(way, h, e):
        s = 1 - 2 * way
        slot = rows_all.at[z_at(-s * h), y_at(-e)]
        return remote(
            slot, slot, z_send.at[way, h, e], z_recv.at[way, h, e], y, z_at(s)
        )

    def z_wait(way, h, e):
        s = 1 - 2 * way
        slot = rows_all.at[z_at(-s * (h + 1)), y_at(-e)]
        remote(
            slot, slot, z_send.at[way, h, e], z_recv.at[way, h, e], y, z_at(s)
        ).wait_recv()

    def far(way, e):
        return (e % 2) == way

    def hid_copy(e):
        there = pl.ds(pl.multiple_of(y_at(e) * cols, cols), cols)
        return remote(
            hid.at[:, there], hid_cols.at[y], hid_send.at[e], hid_recv.at[e], y_at(e), z
        )

    def w_copy(e):
        there = pl.ds(pl.multiple_of(y_at(e) * cols, cols), cols)
        return remote(
            wo_hbm.at[:, there], w_cols.at[y], w_send.at[e], w_recv.at[e], y_at(e), z
        )

    for e in PEERS:
        y_copy(e).start()
    for way in range(2):
        z_copy(way, 0, 0).start()
    for e in PEERS:
        hid_copy(e).start()
    for e in PEERS:
        w_copy(e).start()
    for e in PEERS:
        y_wait(e)
        for way in range(2):
            z_copy(way, 0, e).start()

    local[3].wait()
    first = start[0]
    row = lax.broadcasted_iota(jnp.int32, (patch, head_size), 0)
    for j, target in ((0, keys), (1, vals)):
        low = stale[j, pl.ds(0, patch), :].astype(jnp.float32)
        high = stale[j, pl.ds(patch, patch), :].astype(jnp.float32)
        target[pl.ds(0, patch), :] = jnp.where(row < first, low, high).astype(
            jnp.bfloat16
        )
    for j in range(3):
        local[j].wait()

    query_scale = math.log2(math.e) / math.sqrt(head_size)

    def project(places):
        pieces = [rows_all[at].reshape(block, width) for at in places]
        merged = jnp.dot(
            pieces[0] if len(pieces) == 1 else jnp.concatenate(pieces, axis=0),
            w_all[...],
            preferred_element_type=jnp.float32,
        )
        q = merged[:, :head_size]
        k = merged[:, head_size : 2 * head_size]
        v = merged[:, 2 * head_size :].astype(jnp.bfloat16)
        q = q * lax.rsqrt(jnp.mean(q * q, axis=-1, keepdims=True) + 1e-06)
        q = (q * (gain[0:1, :] * query_scale)).astype(jnp.bfloat16)
        k = k * lax.rsqrt(jnp.mean(k * k, axis=-1, keepdims=True) + 1e-06)
        k = (k * gain[1:2, :]).astype(jnp.bfloat16)
        for i, at in enumerate(places):
            here = slice(i * block, (i + 1) * block)
            there = pl.ds(pl.multiple_of(patch + at * block, block), block)
            queries[at] = q[here]
            keys[there, :] = k[here]
            vals[there, :] = v[here]

    project([z])

    def hop(h, carry):
        for e in (0, *PEERS):
            for way in range(2):
                z_wait(way, h - 1, e)
                if far(way, e):
                    z_copy(way, h, e).start()
                else:

                    @pl.when(h < 3)
                    def _():
                        z_copy(way, h, e).start()

        project([z_at(-h), z_at(h)])
        return carry

    lax.fori_loop(1, 4, hop, 0)
    for e in (0, *PEERS):
        z_wait(e % 2, 3, e)
    project([z_at(4)])

    def head_copy(i, e):
        mine = heads.at[z_at(ORDER[i]), y]
        return remote(mine, mine, head_send.at[i, e], head_recv.at[i, e], y_at(e), z)

    def attend(i):
        at = z_at(ORDER[i])
        scores = lax.dot_general(
            queries[at],
            keys[...],
            (((1,), (1,)), ((), ())),
            preferred_element_type=jnp.float32,
        )
        highest = jnp.max(scores, axis=-1, keepdims=True)
        raised = jnp.exp2(scores - highest)
        total = jnp.sum(raised, axis=-1, keepdims=True)
        mixed_values = jnp.dot(
            raised.astype(jnp.bfloat16), vals[...], preferred_element_type=jnp.float32
        )
        heads[at, y] = (mixed_values / total).astype(jnp.bfloat16)
        for e in PEERS:
            head_copy(i, e).start()

    def ring_copy(way, part, k):
        return remote(
            part_out.at[way, part, k - 1],
            part_in.at[way, part, k - 1],
            ring_send.at[way, part, k - 1],
            ring_recv.at[way, part, k - 1],
            y,
            z_at(1 - 2 * way),
        )

    def length(way, part):
        return 4 if way == part else 3

    def finish(i):
        offset = ORDER[i]
        at = z_at(offset)
        for e in PEERS:
            slot = heads.at[at, y_at(-e)]
            remote(
                slot, slot, head_send.at[i, e], head_recv.at[i, e], y_at(e), z
            ).wait_recv()
        four = jnp.concatenate([heads[at, yy] for yy in range(NY)], axis=1)
        summed = jnp.dot(
            four,
            w_cols[...].reshape(NY * head_size, cols),
            preferred_element_type=jnp.float32,
        )
        pieces = [summed[:half], summed[half:]]
        k = abs(offset)
        ways = (0, 1) if k in (0, 4) else ((0,) if offset > 0 else (1,))
        for way in ways:
            for part in range(2):
                if k > length(way, part):
                    continue
                if k < length(way, part):
                    ring_copy(way, part, k + 1).wait_recv()
                    added = pieces[part] + part_in[way, part, k].astype(jnp.float32)
                else:
                    added = pieces[part]
                if k > 0:
                    part_out[way, part, k - 1] = added.astype(jnp.bfloat16)
                    ring_copy(way, part, k).start()
                else:
                    pieces[part] = added
        return pieces

    blocks = len(ORDER)
    ahead = 2
    pieces = None
    for i in range(blocks + ahead):
        if i < blocks:
            attend(i)
        if i == ahead:
            for e in PEERS:
                slot = w_cols.at[y_at(-e)]
                remote(slot, slot, w_send.at[e], w_recv.at[e], y_at(e), z).wait_recv()
                slot = hid_cols.at[y_at(-e)]
                remote(
                    slot, slot, hid_send.at[e], hid_recv.at[e], y_at(e), z
                ).wait_recv()
            local[4].wait()
        if i >= ahead:
            pieces = finish(i - ahead)

    def out_copy(yy):
        return remote(
            out_rows.at[yy],
            out.at[:, my_cols],
            out_send.at[yy],
            out_recv.at[y],
            yy,
            z,
            after,
        )

    gate = mod[2:3, my_cols]
    for yy in range(NY):
        total = pieces[yy // 2][(yy % 2) * own : (yy % 2 + 1) * own]
        layer_out = hid_cols[yy].astype(jnp.float32) + gate * total
        out_rows[yy] = layer_out.astype(jnp.bfloat16)
        out_copy(yy).start()

    for e in PEERS:
        y_copy(e).wait_send()
        hid_copy(e).wait_send()
        w_copy(e).wait_send()
    for e in range(NY):
        for way in range(2):
            for h in range(4 if far(way, e) else 3):
                z_copy(way, h, e).wait_send()
    for i in range(blocks):
        for e in PEERS:
            head_copy(i, e).wait_send()
    for way in range(2):
        for part in range(2):
            for k in range(1, length(way, part) + 1):
                ring_copy(way, part, k).wait_send()
    for yy in range(NY):
        out_copy(yy).wait_send()
    for yy in range(NY):
        slot = out.at[:, pl.ds(yy * cols, cols)]
        remote(
            out_rows.at[yy], slot, out_send.at[yy], out_recv.at[yy], yy, z, after
        ).wait_recv()


def per_device(sections, hidden, modulation, w_qkv, qk_gain, w_out, stale_kv, patch_start):
    own, width = hidden.shape[1:]
    head_size = qk_gain.shape[2]
    clip = stale_kv.shape[2]
    block = NY * own
    cols = width // NY
    bf16 = jnp.bfloat16
    dma = pltpu.SemaphoreType.DMA
    vmem = pl.BlockSpec(memory_space=pltpu.VMEM)
    anywhere = pl.BlockSpec(memory_space=pl.ANY)
    smem = pl.BlockSpec(memory_space=pltpu.SMEM)
    received = pl.pallas_call(
        functools.partial(kernel, sections),
        out_shape=jax.ShapeDtypeStruct((own, width), bf16),
        in_specs=[vmem, vmem, anywhere, vmem, anywhere, anywhere, smem],
        out_specs=vmem,
        scratch_shapes=[
            pltpu.VMEM((NZ, NY, own, width), bf16),
            pltpu.VMEM((width, 3 * head_size), bf16),
            pltpu.VMEM((NY, head_size, cols), bf16),
            pltpu.VMEM((2, clip, head_size), bf16),
            pltpu.VMEM((clip, head_size), bf16),
            pltpu.VMEM((clip, head_size), bf16),
            pltpu.VMEM((NZ, block, head_size), bf16),
            pltpu.VMEM((NZ, NY, block, head_size), bf16),
            pltpu.VMEM((2, 2, 4, block // 2, cols), bf16),
            pltpu.VMEM((2, 2, 4, block // 2, cols), bf16),
            pltpu.VMEM((NY, own, cols), bf16),
            pltpu.VMEM((NY, own, cols), bf16),
            dma((5,)),
            dma((NY,)),
            dma((NY,)),
            dma((NY,)),
            dma((NY,)),
            dma((NY,)),
            dma((NY,)),
            dma((2, 4, NY)),
            dma((2, 4, NY)),
            dma((NZ, NY)),
            dma((NZ, NY)),
            dma((2, 2, 4)),
            dma((2, 2, 4)),
            dma((NY,)),
            dma((NY,)),
        ],
        compiler_params=pltpu.CompilerParams(
            collective_id=0, has_side_effects=True, vmem_limit_bytes=48 << 20
        ),
    )(
        hidden[0],
        modulation[0],
        jnp.transpose(w_qkv[0], (1, 0, 2)),
        qk_gain[0],
        w_out[0],
        stale_kv[0],
        patch_start,
    )
    return received[None]


def solution(mesh):
    in_specs = (
        P("section", "seq", None),
        P("section", None, None),
        P("section", None, None, "seq"),
        P("section", None, None),
        P("section", "seq", None),
        P("section", None, None, "seq"),
        P("section"),
    )
    out_specs = P("section", "seq", None)
    return jax.shard_map(
        functools.partial(per_device, mesh.shape["section"]),
        mesh=mesh,
        in_specs=in_specs,
        out_specs=out_specs,
        check_vma=False,
    )
```

```python
import functools
import math

import jax
import jax.numpy as jnp
from jax import lax
from jax.experimental import pallas as pl
from jax.experimental.pallas import tpu as pltpu
from jax.sharding import PartitionSpec as P

MESH = pl.DeviceIdType.MESH
NY = 4
NZ = 8
PEERS = (1, 3, 2)
ORDER = (4, 3, -3, 2, -2, 1, -1, 0)
PARTS = 2
ARRIVALS = (
    (1, 0, 0, 0), (0, 0, 1, 0), (0, 0, 1, 1), (3, 0, 0, 0), (0, 1, 1, 0), (0, 1, 1, 1),
    (2, 0, 0, 0), (1, 0, 1, 0), (1, 0, 1, 1), (1, 1, 0, 0), (0, 0, 2, 0), (0, 0, 2, 1),
    (3, 1, 0, 0), (3, 0, 1, 0), (3, 0, 1, 1), (0, 1, 2, 0), (0, 1, 2, 1), (2, 1, 0, 0),
    (2, 0, 1, 0), (1, 0, 2, 0), (2, 0, 1, 1), (1, 0, 2, 1), (1, 1, 1, 0), (1, 1, 1, 1),
    (0, 0, 3, 0), (0, 0, 3, 1), (3, 1, 1, 0), (3, 1, 1, 1), (3, 0, 2, 0), (3, 0, 2, 1),
    (0, 1, 3, 0), (0, 1, 3, 1), (2, 1, 1, 0), (2, 1, 1, 1), (1, 0, 3, 0), (1, 0, 3, 1),
    (2, 0, 2, 0), (2, 0, 2, 1), (1, 1, 2, 0), (1, 1, 2, 1), (0, 0, 4, 0), (3, 1, 2, 1),
    (3, 0, 3, 1), (3, 1, 2, 0), (3, 0, 3, 0), (2, 1, 2, 1), (0, 1, 4, 0), (1, 0, 4, 1),
    (2, 0, 3, 1), (2, 1, 2, 0), (1, 1, 3, 1), (2, 0, 3, 0), (1, 1, 3, 0), (3, 1, 3, 1),
    (3, 0, 4, 1), (3, 1, 3, 0), (2, 1, 3, 0), (2, 1, 3, 1), (1, 1, 4, 1), (2, 0, 4, 0),
    (3, 1, 4, 1), (2, 1, 4, 0),
)


def kernel(
    sections,
    hid_hbm,
    mod_hbm,
    wq_hbm,
    gain_hbm,
    wo_hbm,
    st_hbm,
    start,
    out,
    hid,
    mod,
    gain,
    rows_all,
    w_all,
    w_cols,
    stale,
    keys,
    vals,
    queries,
    heads,
    part_out,
    part_in,
    hid_cols,
    out_rows,
    local_sem,
    y_send,
    y_recv,
    hid_send,
    hid_recv,
    w_send,
    w_recv,
    z_send,
    z_recv,
    head_send,
    head_recv,
    ring_send,
    ring_recv,
    out_send,
    out_recv,
):
    own, width = hid.shape
    head_size = gain.shape[1]
    block = NY * own
    cols = width // NY
    patch = block * NZ
    section = lax.axis_index("section")
    place = lax.axis_index("seq")
    y = place // NZ
    z = place % NZ
    after = (section + 1) % sections
    before = (section + sections - 1) % sections

    y_near = [(y + distance) % NY for distance in range(NY)]
    z_near = [(z + distance) % NZ for distance in range(NZ)]

    def y_at(distance):
        return y_near[distance % NY]

    def z_at(distance):
        return z_near[distance % NZ]

    def remote(src, dst, send, recv, yy, zz, sec=section):
        return pltpu.make_async_remote_copy(
            src_ref=src,
            dst_ref=dst,
            send_sem=send,
            recv_sem=recv,
            device_id=(sec, yy * NZ + zz),
            device_id_type=MESH,
        )

    first_local = [
        pltpu.make_async_copy(src, dst, local_sem.at[5 + j])
        for j, (src, dst) in enumerate(
            ((hid_hbm, hid), (mod_hbm, mod), (gain_hbm, gain))
        )
    ]
    for copy in first_local:
        copy.start()
    local = [
        pltpu.make_async_copy(
            wq_hbm.at[j], w_all.at[:, pl.ds(j * head_size, head_size)], local_sem.at[j]
        )
        for j in range(3)
    ]
    local.append(pltpu.make_async_copy(st_hbm, stale, local_sem.at[3]))
    my_cols = pl.ds(pl.multiple_of(y * cols, cols), cols)
    local.append(
        pltpu.make_async_copy(wo_hbm.at[:, my_cols], w_cols.at[y], local_sem.at[4])
    )
    for copy in local:
        copy.start()

    barrier = pltpu.get_barrier_semaphore()
    partners = [(section, y_at(e) * NZ + z) for e in PEERS]
    partners += [(section, y * NZ + z_at(s)) for s in (1, -1)]
    partners += [(after, yy * NZ + z) for yy in range(NY)]
    partners += [(before, yy * NZ + z) for yy in range(NY)]
    for partner in partners:
        pl.semaphore_signal(barrier, inc=1, device_id=partner, device_id_type=MESH)

    for copy in first_local:
        copy.wait()
    values = hid[...].astype(jnp.float32)
    average = jnp.mean(values, axis=-1, keepdims=True)
    centred = values - average
    spread = jnp.mean(centred * centred, axis=-1, keepdims=True)
    scale = lax.rsqrt(spread + 1e-06)
    piece = width // PARTS

    def modulate(p):
        here = slice(p * piece, (p + 1) * piece)
        normed = centred[:, here] * scale
        mixed = normed * (1.0 + mod[1, :, here]) + mod[0, :, here]
        rows_all[z, p, y] = mixed.astype(jnp.bfloat16)

    modulate(0)
    pl.semaphore_wait(barrier, len(partners))

    def y_copy(e, p):
        mine = rows_all.at[z, p, y]
        return remote(mine, mine, y_send.at[e, p], y_recv.at[e, p], y_at(e), z)

    def y_wait(e, p):
        slot = rows_all.at[z, p, y_at(-e)]
        remote(slot, slot, y_send.at[e, p], y_recv.at[e, p], y_at(e), z).wait_recv()

    def z_copy(way, h, e, p):
        s = 1 - 2 * way
        slot = rows_all.at[z_at(-s * h), p, y_at(-e)]
        sems = (z_send.at[way, h, e, p], z_recv.at[way, h, e, p])
        return remote(slot, slot, *sems, y, z_at(s))

    def z_wait(way, h, e, p):
        s = 1 - 2 * way
        slot = rows_all.at[z_at(-s * (h + 1)), p, y_at(-e)]
        sems = (z_send.at[way, h, e, p], z_recv.at[way, h, e, p])
        remote(slot, slot, *sems, y, z_at(s)).wait_recv()

    def reach(way, e):
        return 4 if (e % 2) == way else 3

    def hid_copy(e):
        there = pl.ds(pl.multiple_of(y_at(e) * cols, cols), cols)
        return remote(
            hid.at[:, there], hid_cols.at[y], hid_send.at[e], hid_recv.at[e], y_at(e), z
        )

    def w_copy(e):
        there = pl.ds(pl.multiple_of(y_at(e) * cols, cols), cols)
        return remote(
            wo_hbm.at[:, there], w_cols.at[y], w_send.at[e], w_recv.at[e], y_at(e), z
        )

    for p in range(PARTS):
        if p:
            modulate(p)
        for way in range(2):
            z_copy(way, 0, 0, p).start()
        if p == 0:
            for e in PEERS:
                y_copy(e, p).start()
    hid_cols[y] = hid[:, my_cols]

    local[3].wait()
    first = start[0]
    row = lax.broadcasted_iota(jnp.int32, (patch, head_size), 0)
    for j, target in ((0, keys), (1, vals)):
        low = stale[j, pl.ds(0, patch), :].astype(jnp.float32)
        high = stale[j, pl.ds(patch, patch), :].astype(jnp.float32)
        target[pl.ds(0, patch), :] = jnp.where(row < first, low, high).astype(
            jnp.bfloat16
        )
    query_scale = math.log2(math.e) / math.sqrt(head_size)

    def project(places):
        merged = 0.0
        for p in range(PARTS):
            rows = [rows_all[at, p].reshape(block, piece) for at in places]
            merged += jnp.dot(
                rows[0] if len(rows) == 1 else jnp.concatenate(rows, axis=0),
                w_all[p * piece : (p + 1) * piece, :],
                preferred_element_type=jnp.float32,
            )
        q = merged[:, :head_size]
        k = merged[:, head_size : 2 * head_size]
        v = merged[:, 2 * head_size :].astype(jnp.bfloat16)
        q = q * lax.rsqrt(jnp.mean(q * q, axis=-1, keepdims=True) + 1e-06)
        q = (q * (gain[0:1, :] * query_scale)).astype(jnp.bfloat16)
        k = k * lax.rsqrt(jnp.mean(k * k, axis=-1, keepdims=True) + 1e-06)
        k = (k * gain[1:2, :]).astype(jnp.bfloat16)
        for i, at in enumerate(places):
            here = slice(i * block, (i + 1) * block)
            there = pl.ds(pl.multiple_of(patch + at * block, block), block)
            queries[at] = q[here]
            keys[there, :] = k[here]
            vals[there, :] = v[here]

    left = [sum(hops == h for _, _, hops, _ in ARRIVALS) for h in range(5)]
    for e, p, h, way in ARRIVALS:
        if h == 0:
            y_wait(e, p)
            for onward in range(2):
                z_copy(onward, 0, e, p).start()
            if p == 0:
                y_copy(e, 0).wait_send()
                y_copy(e, 1).start()
        else:
            z_wait(way, h - 1, e, p)
            if h < reach(way, e):
                z_copy(way, h, e, p).start()
        left[h] -= 1
        if left[h]:
            continue
        if h == 0:
            for peer in PEERS:
                w_copy(peer).start()
            for peer in PEERS:
                hid_copy(peer).start()
            for j in range(3):
                local[j].wait()
            project([z])
        elif h == 4:
            project([z_at(4)])
        else:
            project([z_at(-h), z_at(h)])

    def head_copy(i, e):
        mine = heads.at[z_at(ORDER[i]), y]
        return remote(mine, mine, head_send.at[i, e], head_recv.at[i, e], y_at(e), z)

    def attend(i):
        at = z_at(ORDER[i])
        scores = lax.dot_general(
            queries[at],
            keys[...],
            (((1,), (1,)), ((), ())),
            preferred_element_type=jnp.float32,
        )
        highest = jnp.max(scores, axis=-1, keepdims=True)
        raised = jnp.exp2(scores - highest)
        total = jnp.sum(raised, axis=-1, keepdims=True)
        mixed_values = jnp.dot(
            raised.astype(jnp.bfloat16), vals[...], preferred_element_type=jnp.float32
        )
        heads[at, y] = (mixed_values / total).astype(jnp.bfloat16)
        for e in PEERS:
            head_copy(i, e).start()

    def ring_copy(way, part, k):
        return remote(
            part_out.at[way, part, k - 1],
            part_in.at[way, part, k - 1],
            ring_send.at[way, part, k - 1],
            ring_recv.at[way, part, k - 1],
            y,
            z_at(1 - 2 * way),
        )

    def length(way, part):
        return 4 if way == part % 2 else 3

    def out_copy(yy):
        return remote(
            out_rows.at[yy],
            out.at[:, my_cols],
            out_send.at[yy],
            out_recv.at[y],
            yy,
            z,
            after,
        )

    gate = mod[2, :, my_cols]

    def layer_rows(part, total):
        for way in range(2):
            ring_copy(way, part, 1).wait_recv()
            total += part_in[way, part, 0].astype(jnp.float32)
        layer_out = hid_cols[part].astype(jnp.float32) + gate * total
        out_rows[part] = layer_out.astype(jnp.bfloat16)
        out_copy(part).start()

    def finish(i):
        offset = ORDER[i]
        at = z_at(offset)
        for e in PEERS:
            slot = heads.at[at, y_at(-e)]
            remote(
                slot, slot, head_send.at[i, e], head_recv.at[i, e], y_at(e), z
            ).wait_recv()
        four = jnp.concatenate([heads[at, yy] for yy in range(NY)], axis=1)
        summed = jnp.dot(
            four,
            w_cols[...].reshape(NY * head_size, cols),
            preferred_element_type=jnp.float32,
        )
        pieces = [summed[part * own : (part + 1) * own] for part in range(NY)]
        k = abs(offset)
        if k == 0:
            for part in range(NY):
                layer_rows(part, pieces[part])
            return
        ways = (0, 1) if k == 4 else ((0,) if offset > 0 else (1,))
        for way in ways:
            for part in (1 - way, 3 - way, way, 2 + way):
                if k > length(way, part):
                    continue
                added = pieces[part]
                if k < length(way, part):
                    ring_copy(way, part, k + 1).wait_recv()
                    added += part_in[way, part, k].astype(jnp.float32)
                part_out[way, part, k - 1] = added.astype(jnp.bfloat16)
                ring_copy(way, part, k).start()

    blocks = len(ORDER)
    ahead = 2
    for i in range(blocks + ahead):
        if i < blocks:
            attend(i)
        if i == ahead:
            for e in PEERS:
                slot = w_cols.at[y_at(-e)]
                remote(slot, slot, w_send.at[e], w_recv.at[e], y_at(e), z).wait_recv()
                slot = hid_cols.at[y_at(-e)]
                remote(
                    slot, slot, hid_send.at[e], hid_recv.at[e], y_at(e), z
                ).wait_recv()
            local[4].wait()
        if i >= ahead:
            finish(i - ahead)

    for e in PEERS:
        y_copy(e, 1).wait_send()
        hid_copy(e).wait_send()
        w_copy(e).wait_send()
    for e in range(NY):
        for way in range(2):
            for h in range(reach(way, e)):
                for p in range(PARTS):
                    z_copy(way, h, e, p).wait_send()
    for i in range(blocks):
        for e in PEERS:
            head_copy(i, e).wait_send()
    for way in range(2):
        for part in range(NY):
            for k in range(1, length(way, part) + 1):
                ring_copy(way, part, k).wait_send()
    for yy in range(NY):
        out_copy(yy).wait_send()
    for yy in range(NY):
        slot = out.at[:, pl.ds(yy * cols, cols)]
        remote(
            out_rows.at[yy], slot, out_send.at[yy], out_recv.at[yy], yy, z, after
        ).wait_recv()


def per_device(sections, hidden, modulation, w_qkv, qk_gain, w_out, stale_kv, patch_start):
    own, width = hidden.shape[1:]
    head_size = qk_gain.shape[2]
    clip = stale_kv.shape[2]
    block = NY * own
    cols = width // NY
    bf16 = jnp.bfloat16
    dma = pltpu.SemaphoreType.DMA
    anywhere = pl.BlockSpec(memory_space=pl.ANY)
    smem = pl.BlockSpec(memory_space=pltpu.SMEM)
    received = pl.pallas_call(
        functools.partial(kernel, sections),
        out_shape=jax.ShapeDtypeStruct((own, width), bf16),
        in_specs=[anywhere] * 6 + [smem],
        out_specs=anywhere,
        scratch_shapes=[
            pltpu.VMEM((own, width), bf16),
            pltpu.VMEM((3, 1, width), jnp.float32),
            pltpu.VMEM((2, head_size), jnp.float32),
            pltpu.VMEM((NZ, PARTS, NY, own, width // PARTS), bf16),
            pltpu.VMEM((width, 3 * head_size), bf16),
            pltpu.VMEM((NY, head_size, cols), bf16),
            pltpu.VMEM((2, clip, head_size), bf16),
            pltpu.VMEM((clip, head_size), bf16),
            pltpu.VMEM((clip, head_size), bf16),
            pltpu.VMEM((NZ, block, head_size), bf16),
            pltpu.VMEM((NZ, NY, block, head_size), bf16),
            pltpu.VMEM((2, NY, 4, own, cols), bf16),
            pltpu.VMEM((2, NY, 4, own, cols), bf16),
            pltpu.VMEM((NY, own, cols), bf16),
            pltpu.VMEM((NY, own, cols), bf16),
            dma((8,)),
            dma((NY, PARTS)),
            dma((NY, PARTS)),
            dma((NY,)),
            dma((NY,)),
            dma((NY,)),
            dma((NY,)),
            dma((2, 4, NY, PARTS)),
            dma((2, 4, NY, PARTS)),
            dma((NZ, NY)),
            dma((NZ, NY)),
            dma((2, NY, 4)),
            dma((2, NY, 4)),
            dma((NY,)),
            dma((NY,)),
        ],
        compiler_params=pltpu.CompilerParams(
            collective_id=0, has_side_effects=True, vmem_limit_bytes=60 << 20
        ),
    )(
        hidden[0],
        jnp.transpose(modulation, (1, 0, 2)),
        jnp.transpose(w_qkv[0], (1, 0, 2)),
        qk_gain[0],
        w_out[0],
        stale_kv[0],
        patch_start,
    )
    return received[None]


def solution(mesh):
    in_specs = (
        P("section", "seq", None),
        P("section", None, None),
        P("section", None, None, "seq"),
        P("section", None, None),
        P("section", "seq", None),
        P("section", None, None, "seq"),
        P("section"),
    )
    out_specs = P("section", "seq", None)
    return jax.shard_map(
        functools.partial(per_device, mesh.shape["section"]),
        mesh=mesh,
        in_specs=in_specs,
        out_specs=out_specs,
        check_vma=False,
    )
```

```python
import functools
import math

import jax
import jax.numpy as jnp
from jax import lax
from jax.experimental import pallas as pl
from jax.experimental.pallas import tpu as pltpu
from jax.sharding import PartitionSpec as P

MESH = pl.DeviceIdType.MESH
NY = 4
NZ = 8
PEERS = (1, 3, 2)
ORDER = (4, 3, -3, 2, -2, 1, -1, 0)
PARTS = 2
ARRIVALS = (
    (1, 0, 0, 0), (0, 0, 1, 0), (0, 0, 1, 1), (3, 0, 0, 0), (0, 1, 1, 0), (0, 1, 1, 1),
    (2, 0, 0, 0), (1, 0, 1, 0), (1, 0, 1, 1), (1, 1, 0, 0), (0, 0, 2, 0), (0, 0, 2, 1),
    (3, 1, 0, 0), (3, 0, 1, 0), (3, 0, 1, 1), (0, 1, 2, 0), (0, 1, 2, 1), (2, 1, 0, 0),
    (2, 0, 1, 0), (1, 0, 2, 0), (2, 0, 1, 1), (1, 0, 2, 1), (1, 1, 1, 0), (1, 1, 1, 1),
    (0, 0, 3, 0), (0, 0, 3, 1), (3, 1, 1, 0), (3, 1, 1, 1), (3, 0, 2, 0), (3, 0, 2, 1),
    (0, 1, 3, 0), (0, 1, 3, 1), (2, 1, 1, 0), (2, 1, 1, 1), (1, 0, 3, 0), (1, 0, 3, 1),
    (2, 0, 2, 0), (2, 0, 2, 1), (1, 1, 2, 0), (1, 1, 2, 1), (0, 0, 4, 0), (3, 1, 2, 1),
    (3, 0, 3, 1), (3, 1, 2, 0), (3, 0, 3, 0), (2, 1, 2, 1), (0, 1, 4, 0), (1, 0, 4, 1),
    (2, 0, 3, 1), (2, 1, 2, 0), (1, 1, 3, 1), (2, 0, 3, 0), (1, 1, 3, 0), (3, 1, 3, 1),
    (3, 0, 4, 1), (3, 1, 3, 0), (2, 1, 3, 0), (2, 1, 3, 1), (1, 1, 4, 1), (2, 0, 4, 0),
    (3, 1, 4, 1), (2, 1, 4, 0),
)


def kernel(
    sections,
    hid_hbm,
    mod_hbm,
    wq_hbm,
    gain_hbm,
    wo_hbm,
    st_hbm,
    start,
    out,
    hid,
    mod,
    gain,
    rows_all,
    w_all,
    w_cols,
    stale,
    keys,
    vals,
    queries,
    heads,
    part_out,
    part_in,
    hid_cols,
    out_rows,
    local_sem,
    y_send,
    y_recv,
    hid_send,
    hid_recv,
    w_send,
    w_recv,
    z_send,
    z_recv,
    head_send,
    head_recv,
    ring_send,
    ring_recv,
    out_send,
    out_recv,
):
    own, width = hid.shape
    head_size = gain.shape[1]
    block = NY * own
    cols = width // NY
    patch = block * NZ
    section = lax.axis_index("section")
    place = lax.axis_index("seq")
    y = place // NZ
    z = place % NZ
    after = (section + 1) % sections
    before = (section + sections - 1) % sections

    y_near = [(y + distance) % NY for distance in range(NY)]
    z_near = [(z + distance) % NZ for distance in range(NZ)]

    def y_at(distance):
        return y_near[distance % NY]

    def z_at(distance):
        return z_near[distance % NZ]

    def remote(src, dst, send, recv, yy, zz, sec=section):
        return pltpu.make_async_remote_copy(
            src_ref=src,
            dst_ref=dst,
            send_sem=send,
            recv_sem=recv,
            device_id=(sec, yy * NZ + zz),
            device_id_type=MESH,
        )

    first_local = [
        pltpu.make_async_copy(src, dst, local_sem.at[5 + j])
        for j, (src, dst) in enumerate(
            ((hid_hbm, hid), (mod_hbm, mod), (gain_hbm, gain))
        )
    ]
    for copy in first_local:
        copy.start()
    local = [
        pltpu.make_async_copy(
            wq_hbm.at[j], w_all.at[:, pl.ds(j * head_size, head_size)], local_sem.at[j]
        )
        for j in range(3)
    ]
    local.append(pltpu.make_async_copy(st_hbm, stale, local_sem.at[3]))
    my_cols = pl.ds(pl.multiple_of(y * cols, cols), cols)
    local.append(
        pltpu.make_async_copy(wo_hbm.at[:, my_cols], w_cols.at[y], local_sem.at[4])
    )
    for copy in local:
        copy.start()

    barrier = pltpu.get_barrier_semaphore()
    partners = [(section, y_at(e) * NZ + z) for e in PEERS]
    partners += [(section, y * NZ + z_at(s)) for s in (1, -1, 2, -2)]
    partners += [(after, yy * NZ + z) for yy in range(NY)]
    partners += [(before, yy * NZ + z) for yy in range(NY)]
    for partner in partners:
        pl.semaphore_signal(barrier, inc=1, device_id=partner, device_id_type=MESH)

    for copy in first_local:
        copy.wait()
    values = hid[...].astype(jnp.float32)
    average = jnp.mean(values, axis=-1, keepdims=True)
    centred = values - average
    spread = jnp.mean(centred * centred, axis=-1, keepdims=True)
    scale = lax.rsqrt(spread + 1e-06)
    piece = width // PARTS

    def modulate(p):
        here = slice(p * piece, (p + 1) * piece)
        normed = centred[:, here] * scale
        mixed = normed * (1.0 + mod[1, :, here]) + mod[0, :, here]
        rows_all[z, p, y] = mixed.astype(jnp.bfloat16)

    modulate(0)
    pl.semaphore_wait(barrier, len(partners))

    def y_copy(e, p):
        mine = rows_all.at[z, p, y]
        return remote(mine, mine, y_send.at[e, p], y_recv.at[e, p], y_at(e), z)

    def y_wait(e, p):
        slot = rows_all.at[z, p, y_at(-e)]
        remote(slot, slot, y_send.at[e, p], y_recv.at[e, p], y_at(e), z).wait_recv()

    def z_copy(way, h, e, p):
        s = 1 - 2 * way
        slot = rows_all.at[z_at(-s * h), p, y_at(-e)]
        sems = (z_send.at[way, h, e, p], z_recv.at[way, h, e, p])
        return remote(slot, slot, *sems, y, z_at(s))

    def z_wait(way, h, e, p):
        s = 1 - 2 * way
        slot = rows_all.at[z_at(-s * (h + 1)), p, y_at(-e)]
        sems = (z_send.at[way, h, e, p], z_recv.at[way, h, e, p])
        remote(slot, slot, *sems, y, z_at(s)).wait_recv()

    def reach(way, e):
        return 4 if (e % 2) == way else 3

    def hid_copy(e):
        there = pl.ds(pl.multiple_of(y_at(e) * cols, cols), cols)
        return remote(
            hid.at[:, there], hid_cols.at[y], hid_send.at[e], hid_recv.at[e], y_at(e), z
        )

    def w_copy(e):
        there = pl.ds(pl.multiple_of(y_at(e) * cols, cols), cols)
        return remote(
            wo_hbm.at[:, there], w_cols.at[y], w_send.at[e], w_recv.at[e], y_at(e), z
        )

    for p in range(PARTS):
        if p:
            modulate(p)
        for way in range(2):
            z_copy(way, 0, 0, p).start()
        if p == 0:
            for e in PEERS:
                y_copy(e, p).start()
    hid_cols[y] = hid[:, my_cols]

    local[3].wait()
    first = start[0]
    row = lax.broadcasted_iota(jnp.int32, (patch, head_size), 0)
    for j, target in ((0, keys), (1, vals)):
        low = stale[j, pl.ds(0, patch), :].astype(jnp.float32)
        high = stale[j, pl.ds(patch, patch), :].astype(jnp.float32)
        target[pl.ds(0, patch), :] = jnp.where(row < first, low, high).astype(
            jnp.bfloat16
        )
    query_scale = math.log2(math.e) / math.sqrt(head_size)

    def project(places):
        merged = 0.0
        for p in range(PARTS):
            rows = [rows_all[at, p].reshape(block, piece) for at in places]
            merged += jnp.dot(
                rows[0] if len(rows) == 1 else jnp.concatenate(rows, axis=0),
                w_all[p * piece : (p + 1) * piece, :],
                preferred_element_type=jnp.float32,
            )
        q = merged[:, :head_size]
        k = merged[:, head_size : 2 * head_size]
        v = merged[:, 2 * head_size :].astype(jnp.bfloat16)
        q = q * lax.rsqrt(jnp.mean(q * q, axis=-1, keepdims=True) + 1e-06)
        q = (q * (gain[0:1, :] * query_scale)).astype(jnp.bfloat16)
        k = k * lax.rsqrt(jnp.mean(k * k, axis=-1, keepdims=True) + 1e-06)
        k = (k * gain[1:2, :]).astype(jnp.bfloat16)
        for i, at in enumerate(places):
            here = slice(i * block, (i + 1) * block)
            there = pl.ds(pl.multiple_of(patch + at * block, block), block)
            queries[at] = q[here]
            keys[there, :] = k[here]
            vals[there, :] = v[here]

    left = [sum(hops == h for _, _, hops, _ in ARRIVALS) for h in range(5)]
    for e, p, h, way in ARRIVALS:
        if h == 0:
            y_wait(e, p)
            for onward in range(2):
                z_copy(onward, 0, e, p).start()
            if p == 0:
                y_copy(e, 0).wait_send()
                y_copy(e, 1).start()
        else:
            z_wait(way, h - 1, e, p)
            if h < reach(way, e):
                z_copy(way, h, e, p).start()
        left[h] -= 1
        if left[h]:
            continue
        if h == 0:
            for peer in PEERS:
                w_copy(peer).start()
            for peer in PEERS:
                hid_copy(peer).start()
            for j in range(3):
                local[j].wait()
            project([z])
        elif h == 4:
            project([z_at(4)])
        else:
            project([z_at(-h), z_at(h)])

    def head_copy(i, e):
        mine = heads.at[z_at(ORDER[i]), y]
        return remote(mine, mine, head_send.at[i, e], head_recv.at[i, e], y_at(e), z)

    def attend(i):
        at = z_at(ORDER[i])
        scores = lax.dot_general(
            queries[at],
            keys[...],
            (((1,), (1,)), ((), ())),
            preferred_element_type=jnp.float32,
        )
        highest = jnp.max(scores, axis=-1, keepdims=True)
        raised = jnp.exp2(scores - highest)
        total = jnp.sum(raised, axis=-1, keepdims=True)
        mixed_values = jnp.dot(
            raised.astype(jnp.bfloat16), vals[...], preferred_element_type=jnp.float32
        )
        heads[at, y] = (mixed_values / total).astype(jnp.bfloat16)
        for e in PEERS:
            head_copy(i, e).start()

    def ring_copy(way, part, k):
        return remote(
            part_out.at[way, part, k - 1],
            part_in.at[way, part, k - 1],
            ring_send.at[way, part, k - 1],
            ring_recv.at[way, part, k - 1],
            y,
            z_at((1 - 2 * way) * (2 if k == 4 else 1)),
        )

    def length(way, part):
        return 4 if way == part % 2 else 3

    def out_copy(yy):
        return remote(
            out_rows.at[yy],
            out.at[:, my_cols],
            out_send.at[yy],
            out_recv.at[y],
            yy,
            z,
            after,
        )

    gate = mod[2, :, my_cols]

    def layer_rows(part, total):
        for way in range(2):
            ring_copy(way, part, 1).wait_recv()
            total += part_in[way, part, 0].astype(jnp.float32)
        layer_out = hid_cols[part].astype(jnp.float32) + gate * total
        out_rows[part] = layer_out.astype(jnp.bfloat16)
        out_copy(part).start()

    def finish(i):
        offset = ORDER[i]
        at = z_at(offset)
        for e in PEERS:
            slot = heads.at[at, y_at(-e)]
            remote(
                slot, slot, head_send.at[i, e], head_recv.at[i, e], y_at(e), z
            ).wait_recv()
        four = jnp.concatenate([heads[at, yy] for yy in range(NY)], axis=1)
        summed = jnp.dot(
            four,
            w_cols[...].reshape(NY * head_size, cols),
            preferred_element_type=jnp.float32,
        )
        pieces = [summed[part * own : (part + 1) * own] for part in range(NY)]
        k = abs(offset)
        if k == 0:
            for part in range(NY):
                layer_rows(part, pieces[part])
            return
        ways = (0, 1) if k == 4 else ((0,) if offset > 0 else (1,))
        for way in ways:
            for part in range(NY):
                if k > length(way, part):
                    continue
                added = pieces[part]
                came = [k + 1] if k < 3 else []
                if k == 2 and length(way, part) == 4:
                    came.append(4)
                for c in came:
                    ring_copy(way, part, c).wait_recv()
                    added += part_in[way, part, c - 1].astype(jnp.float32)
                part_out[way, part, k - 1] = added.astype(jnp.bfloat16)
                ring_copy(way, part, k).start()

    blocks = len(ORDER)
    ahead = 3
    for i in range(blocks + ahead):
        if i < blocks:
            attend(i)
        if i == ahead:
            for e in PEERS:
                slot = w_cols.at[y_at(-e)]
                remote(slot, slot, w_send.at[e], w_recv.at[e], y_at(e), z).wait_recv()
                slot = hid_cols.at[y_at(-e)]
                remote(
                    slot, slot, hid_send.at[e], hid_recv.at[e], y_at(e), z
                ).wait_recv()
            local[4].wait()
        if i >= ahead:
            finish(i - ahead)

    for e in PEERS:
        y_copy(e, 1).wait_send()
        hid_copy(e).wait_send()
        w_copy(e).wait_send()
    for e in range(NY):
        for way in range(2):
            for h in range(reach(way, e)):
                for p in range(PARTS):
                    z_copy(way, h, e, p).wait_send()
    for i in range(blocks):
        for e in PEERS:
            head_copy(i, e).wait_send()
    for way in range(2):
        for part in range(NY):
            for k in range(1, length(way, part) + 1):
                ring_copy(way, part, k).wait_send()
    for yy in range(NY):
        out_copy(yy).wait_send()
    for yy in range(NY):
        slot = out.at[:, pl.ds(yy * cols, cols)]
        remote(
            out_rows.at[yy], slot, out_send.at[yy], out_recv.at[yy], yy, z, after
        ).wait_recv()


def per_device(sections, hidden, modulation, w_qkv, qk_gain, w_out, stale_kv, patch_start):
    own, width = hidden.shape[1:]
    head_size = qk_gain.shape[2]
    clip = stale_kv.shape[2]
    block = NY * own
    cols = width // NY
    bf16 = jnp.bfloat16
    dma = pltpu.SemaphoreType.DMA
    anywhere = pl.BlockSpec(memory_space=pl.ANY)
    smem = pl.BlockSpec(memory_space=pltpu.SMEM)
    received = pl.pallas_call(
        functools.partial(kernel, sections),
        out_shape=jax.ShapeDtypeStruct((own, width), bf16),
        in_specs=[anywhere] * 6 + [smem],
        out_specs=anywhere,
        scratch_shapes=[
            pltpu.VMEM((own, width), bf16),
            pltpu.VMEM((3, 1, width), jnp.float32),
            pltpu.VMEM((2, head_size), jnp.float32),
            pltpu.VMEM((NZ, PARTS, NY, own, width // PARTS), bf16),
            pltpu.VMEM((width, 3 * head_size), bf16),
            pltpu.VMEM((NY, head_size, cols), bf16),
            pltpu.VMEM((2, clip, head_size), bf16),
            pltpu.VMEM((clip, head_size), bf16),
            pltpu.VMEM((clip, head_size), bf16),
            pltpu.VMEM((NZ, block, head_size), bf16),
            pltpu.VMEM((NZ, NY, block, head_size), bf16),
            pltpu.VMEM((2, NY, 4, own, cols), bf16),
            pltpu.VMEM((2, NY, 4, own, cols), bf16),
            pltpu.VMEM((NY, own, cols), bf16),
            pltpu.VMEM((NY, own, cols), bf16),
            dma((8,)),
            dma((NY, PARTS)),
            dma((NY, PARTS)),
            dma((NY,)),
            dma((NY,)),
            dma((NY,)),
            dma((NY,)),
            dma((2, 4, NY, PARTS)),
            dma((2, 4, NY, PARTS)),
            dma((NZ, NY)),
            dma((NZ, NY)),
            dma((2, NY, 4)),
            dma((2, NY, 4)),
            dma((NY,)),
            dma((NY,)),
        ],
        compiler_params=pltpu.CompilerParams(
            collective_id=0, has_side_effects=True, vmem_limit_bytes=60 << 20
        ),
    )(
        hidden[0],
        jnp.transpose(modulation, (1, 0, 2)),
        jnp.transpose(w_qkv[0], (1, 0, 2)),
        qk_gain[0],
        w_out[0],
        stale_kv[0],
        patch_start,
    )
    return received[None]


def solution(mesh):
    in_specs = (
        P("section", "seq", None),
        P("section", None, None),
        P("section", None, None, "seq"),
        P("section", None, None),
        P("section", "seq", None),
        P("section", None, None, "seq"),
        P("section"),
    )
    out_specs = P("section", "seq", None)
    return jax.shard_map(
        functools.partial(per_device, mesh.shape["section"]),
        mesh=mesh,
        in_specs=in_specs,
        out_specs=out_specs,
        check_vma=False,
    )
```

```python
import functools
import math

import jax
import jax.numpy as jnp
from jax import lax
from jax.experimental import pallas as pl
from jax.experimental.pallas import tpu as pltpu
from jax.sharding import PartitionSpec as P

MESH = pl.DeviceIdType.MESH
NY = 4
NZ = 8
PEERS = (1, 3, 2)
ORDER = (4, 3, -3, 2, -2, 1, -1, 0)
PARTS = 2
ARRIVALS = (
    (1, 0, 0, 0), (0, 0, 1, 0), (0, 0, 1, 1), (3, 0, 0, 0), (0, 1, 1, 0), (0, 1, 1, 1),
    (2, 0, 0, 0), (1, 0, 1, 0), (1, 0, 1, 1), (1, 1, 0, 0), (0, 0, 2, 0), (0, 0, 2, 1),
    (3, 1, 0, 0), (3, 0, 1, 0), (3, 0, 1, 1), (0, 1, 2, 0), (0, 1, 2, 1), (2, 1, 0, 0),
    (2, 0, 1, 0), (1, 0, 2, 0), (2, 0, 1, 1), (1, 0, 2, 1), (1, 1, 1, 0), (1, 1, 1, 1),
    (0, 0, 3, 0), (0, 0, 3, 1), (3, 1, 1, 0), (3, 1, 1, 1), (3, 0, 2, 0), (3, 0, 2, 1),
    (0, 1, 3, 0), (0, 1, 3, 1), (2, 1, 1, 0), (2, 1, 1, 1), (1, 0, 3, 0), (1, 0, 3, 1),
    (2, 0, 2, 0), (2, 0, 2, 1), (1, 1, 2, 0), (1, 1, 2, 1), (0, 0, 4, 0), (3, 1, 2, 1),
    (3, 0, 3, 1), (3, 1, 2, 0), (3, 0, 3, 0), (2, 1, 2, 1), (0, 1, 4, 0), (1, 0, 4, 1),
    (2, 0, 3, 1), (2, 1, 2, 0), (1, 1, 3, 1), (2, 0, 3, 0), (1, 1, 3, 0), (3, 1, 3, 1),
    (3, 0, 4, 1), (3, 1, 3, 0), (2, 1, 3, 0), (2, 1, 3, 1), (1, 1, 4, 1), (2, 0, 4, 0),
    (3, 1, 4, 1), (2, 1, 4, 0),
)


def kernel(
    sections,
    hid_hbm,
    mod_hbm,
    wq_hbm,
    gain_hbm,
    wo_hbm,
    st_hbm,
    start,
    out,
    hid,
    mod,
    gain,
    rows_all,
    w_all,
    w_cols,
    stale,
    keys,
    vals,
    queries,
    heads,
    part_out,
    part_in,
    hid_cols,
    out_rows,
    local_sem,
    y_send,
    y_recv,
    hid_send,
    hid_recv,
    w_send,
    w_recv,
    z_send,
    z_recv,
    head_send,
    head_recv,
    ring_send,
    ring_recv,
    out_send,
    out_recv,
):
    own, width = hid.shape
    head_size = gain.shape[1]
    block = NY * own
    cols = width // NY
    patch = block * NZ
    section = lax.axis_index("section")
    place = lax.axis_index("seq")
    y = place // NZ
    z = place % NZ
    after = (section + 1) % sections
    before = (section + sections - 1) % sections

    y_near = [(y + distance) % NY for distance in range(NY)]
    z_near = [(z + distance) % NZ for distance in range(NZ)]

    def y_at(distance):
        return y_near[distance % NY]

    def z_at(distance):
        return z_near[distance % NZ]

    def remote(src, dst, send, recv, yy, zz, sec=section):
        return pltpu.make_async_remote_copy(
            src_ref=src,
            dst_ref=dst,
            send_sem=send,
            recv_sem=recv,
            device_id=(sec, yy * NZ + zz),
            device_id_type=MESH,
        )

    first_local = [
        pltpu.make_async_copy(src, dst, local_sem.at[5 + j])
        for j, (src, dst) in enumerate(
            ((hid_hbm, hid), (mod_hbm, mod), (gain_hbm, gain))
        )
    ]
    for copy in first_local:
        copy.start()
    local = [
        pltpu.make_async_copy(
            wq_hbm.at[j], w_all.at[:, pl.ds(j * head_size, head_size)], local_sem.at[j]
        )
        for j in range(3)
    ]
    local.append(pltpu.make_async_copy(st_hbm, stale, local_sem.at[3]))
    my_cols = pl.ds(pl.multiple_of(y * cols, cols), cols)
    local.append(
        pltpu.make_async_copy(wo_hbm.at[:, my_cols], w_cols.at[y], local_sem.at[4])
    )
    for copy in local:
        copy.start()

    barrier = pltpu.get_barrier_semaphore()
    partners = [(section, y_at(e) * NZ + z) for e in PEERS]
    partners += [(section, y * NZ + z_at(s)) for s in (1, -1, 2, -2)]
    partners += [(after, yy * NZ + z) for yy in range(NY)]
    partners += [(before, yy * NZ + z) for yy in range(NY)]
    for partner in partners:
        pl.semaphore_signal(barrier, inc=1, device_id=partner, device_id_type=MESH)

    for copy in first_local:
        copy.wait()
    values = hid[...].astype(jnp.float32)
    average = jnp.mean(values, axis=-1, keepdims=True)
    centred = values - average
    spread = jnp.mean(centred * centred, axis=-1, keepdims=True)
    scale = lax.rsqrt(spread + 1e-06)
    piece = width // PARTS

    def modulate(p):
        here = slice(p * piece, (p + 1) * piece)
        normed = centred[:, here] * scale
        mixed = normed * (1.0 + mod[1, :, here]) + mod[0, :, here]
        rows_all[z, p, y] = mixed.astype(jnp.bfloat16)

    modulate(0)
    pl.semaphore_wait(barrier, len(partners))

    def y_copy(e, p):
        mine = rows_all.at[z, p, y]
        return remote(mine, mine, y_send.at[e, p], y_recv.at[e, p], y_at(e), z)

    def y_wait(e, p):
        slot = rows_all.at[z, p, y_at(-e)]
        remote(slot, slot, y_send.at[e, p], y_recv.at[e, p], y_at(e), z).wait_recv()

    def z_copy(way, h, e, p):
        s = 1 - 2 * way
        slot = rows_all.at[z_at(-s * h), p, y_at(-e)]
        sems = (z_send.at[way, h, e, p], z_recv.at[way, h, e, p])
        return remote(slot, slot, *sems, y, z_at(s))

    def z_wait(way, h, e, p):
        s = 1 - 2 * way
        slot = rows_all.at[z_at(-s * (h + 1)), p, y_at(-e)]
        sems = (z_send.at[way, h, e, p], z_recv.at[way, h, e, p])
        remote(slot, slot, *sems, y, z_at(s)).wait_recv()

    def reach(way, e):
        return 4 if (e % 2) == way else 3

    def hid_copy(e):
        there = pl.ds(pl.multiple_of(y_at(e) * cols, cols), cols)
        return remote(
            hid.at[:, there], hid_cols.at[y], hid_send.at[e], hid_recv.at[e], y_at(e), z
        )

    def w_copy(e):
        there = pl.ds(pl.multiple_of(y_at(e) * cols, cols), cols)
        return remote(
            wo_hbm.at[:, there], w_cols.at[y], w_send.at[e], w_recv.at[e], y_at(e), z
        )

    for p in range(PARTS):
        if p:
            modulate(p)
        for way in range(2):
            z_copy(way, 0, 0, p).start()
        if p == 0:
            for e in PEERS:
                y_copy(e, p).start()
    hid_cols[y] = hid[:, my_cols]

    local[3].wait()
    first = start[0]
    row = lax.broadcasted_iota(jnp.int32, (patch, head_size), 0)
    for j, target in ((0, keys), (1, vals)):
        low = stale[j, pl.ds(0, patch), :].astype(jnp.float32)
        high = stale[j, pl.ds(patch, patch), :].astype(jnp.float32)
        target[pl.ds(0, patch), :] = jnp.where(row < first, low, high).astype(
            jnp.bfloat16
        )
    query_scale = math.log2(math.e) / math.sqrt(head_size)

    def project(places):
        merged = 0.0
        for p in range(PARTS):
            rows = [rows_all[at, p].reshape(block, piece) for at in places]
            merged += jnp.dot(
                rows[0] if len(rows) == 1 else jnp.concatenate(rows, axis=0),
                w_all[p * piece : (p + 1) * piece, :],
                preferred_element_type=jnp.float32,
            )
        q = merged[:, :head_size]
        k = merged[:, head_size : 2 * head_size]
        v = merged[:, 2 * head_size :].astype(jnp.bfloat16)
        q = q * lax.rsqrt(jnp.mean(q * q, axis=-1, keepdims=True) + 1e-06)
        q = (q * (gain[0:1, :] * query_scale)).astype(jnp.bfloat16)
        k = k * lax.rsqrt(jnp.mean(k * k, axis=-1, keepdims=True) + 1e-06)
        k = (k * gain[1:2, :]).astype(jnp.bfloat16)
        for i, at in enumerate(places):
            here = slice(i * block, (i + 1) * block)
            there = pl.ds(pl.multiple_of(patch + at * block, block), block)
            queries[at] = q[here]
            keys[there, :] = k[here]
            vals[there, :] = v[here]

    left = [sum(hops == h for _, _, hops, _ in ARRIVALS) for h in range(5)]
    for e, p, h, way in ARRIVALS:
        if h == 0:
            y_wait(e, p)
            for onward in range(2):
                z_copy(onward, 0, e, p).start()
            if p == 0:
                y_copy(e, 0).wait_send()
                y_copy(e, 1).start()
        else:
            z_wait(way, h - 1, e, p)
            if h < reach(way, e):
                z_copy(way, h, e, p).start()
        left[h] -= 1
        if left[h]:
            continue
        if h == 0:
            for peer in PEERS:
                w_copy(peer).start()
            for peer in PEERS:
                hid_copy(peer).start()
            for j in range(3):
                local[j].wait()
            project([z])
        elif h == 4:
            project([z_at(4)])
        else:
            project([z_at(-h), z_at(h)])

    def head_copy(i, e):
        mine = heads.at[z_at(ORDER[i]), y]
        return remote(mine, mine, head_send.at[i, e], head_recv.at[i, e], y_at(e), z)

    def attend(i):
        at = z_at(ORDER[i])
        scores = lax.dot_general(
            queries[at],
            keys[...],
            (((1,), (1,)), ((), ())),
            preferred_element_type=jnp.float32,
        )
        highest = jnp.max(scores, axis=-1, keepdims=True)
        raised = jnp.exp2(scores - highest)
        total = jnp.sum(raised, axis=-1, keepdims=True)
        mixed_values = jnp.dot(
            raised.astype(jnp.bfloat16), vals[...], preferred_element_type=jnp.float32
        )
        heads[at, y] = (mixed_values / total).astype(jnp.bfloat16)
        for e in PEERS:
            head_copy(i, e).start()

    def ring_copy(way, part, k):
        return remote(
            part_out.at[way, part, k - 1],
            part_in.at[way, part, k - 1],
            ring_send.at[way, part, k - 1],
            ring_recv.at[way, part, k - 1],
            y,
            z_at((1 - 2 * way) * (2 if k == 4 else 1)),
        )

    def length(way, part):
        return 4 if way == part % 2 else 3

    def out_copy(yy):
        return remote(
            out_rows.at[yy],
            out.at[:, my_cols],
            out_send.at[yy],
            out_recv.at[y],
            yy,
            z,
            after,
        )

    gate = mod[2, :, my_cols]

    def layer_rows(part, total):
        for way in range(2):
            ring_copy(way, part, 1).wait_recv()
            total += part_in[way, part, 0].astype(jnp.float32)
        layer_out = hid_cols[part].astype(jnp.float32) + gate * total
        out_rows[part] = layer_out.astype(jnp.bfloat16)
        out_copy(part).start()

    def finish(i):
        offset = ORDER[i]
        at = z_at(offset)
        for e in PEERS:
            slot = heads.at[at, y_at(-e)]
            remote(
                slot, slot, head_send.at[i, e], head_recv.at[i, e], y_at(e), z
            ).wait_recv()
        four = jnp.concatenate([heads[at, yy] for yy in range(NY)], axis=1)
        summed = jnp.dot(
            four,
            w_cols[...].reshape(NY * head_size, cols),
            preferred_element_type=jnp.float32,
        )
        pieces = [summed[part * own : (part + 1) * own] for part in range(NY)]
        k = abs(offset)
        if k == 0:
            for part in range(NY):
                layer_rows(part, pieces[part])
            return
        ways = (0, 1) if k == 4 else ((0,) if offset > 0 else (1,))
        for way in ways:
            for part in range(NY):
                if k > length(way, part):
                    continue
                added = pieces[part]
                came = [k + 1] if k < 3 else []
                if k == 2 and length(way, part) == 4:
                    came.append(4)
                for c in came:
                    ring_copy(way, part, c).wait_recv()
                    added += part_in[way, part, c - 1].astype(jnp.float32)
                part_out[way, part, k - 1] = added.astype(jnp.bfloat16)
                ring_copy(way, part, k).start()

    blocks = len(ORDER)
    ahead = 3
    for i in range(blocks + ahead):
        if i < blocks:
            attend(i)
        if i == ahead:
            for e in PEERS:
                slot = w_cols.at[y_at(-e)]
                remote(slot, slot, w_send.at[e], w_recv.at[e], y_at(e), z).wait_recv()
                slot = hid_cols.at[y_at(-e)]
                remote(
                    slot, slot, hid_send.at[e], hid_recv.at[e], y_at(e), z
                ).wait_recv()
            local[4].wait()
        if i >= ahead:
            finish(i - ahead)

    for e in PEERS:
        y_copy(e, 1).wait_send()
        hid_copy(e).wait_send()
        w_copy(e).wait_send()
    for e in range(NY):
        for way in range(2):
            for h in range(reach(way, e)):
                for p in range(PARTS):
                    z_copy(way, h, e, p).wait_send()
    for i in range(blocks):
        for e in PEERS:
            head_copy(i, e).wait_send()
    for way in range(2):
        for part in range(NY):
            for k in range(1, length(way, part) + 1):
                ring_copy(way, part, k).wait_send()
    for yy in range(NY):
        out_copy(yy).wait_send()
    for yy in range(NY):
        slot = out.at[:, pl.ds(yy * cols, cols)]
        remote(
            out_rows.at[yy], slot, out_send.at[yy], out_recv.at[yy], yy, z, after
        ).wait_recv()


def per_device(sections, hidden, modulation, w_qkv, qk_gain, w_out, stale_kv, patch_start):
    own, width = hidden.shape[1:]
    head_size = qk_gain.shape[2]
    clip = stale_kv.shape[2]
    block = NY * own
    cols = width // NY
    bf16 = jnp.bfloat16
    dma = pltpu.SemaphoreType.DMA
    hbm = pl.BlockSpec(memory_space=pltpu.HBM)
    vmem = pl.BlockSpec(memory_space=pltpu.VMEM)
    smem = pl.BlockSpec(memory_space=pltpu.SMEM)
    received = pl.pallas_call(
        functools.partial(kernel, sections),
        out_shape=jax.ShapeDtypeStruct((own, width), bf16),
        in_specs=[hbm] * 6 + [smem],
        out_specs=vmem,
        scratch_shapes=[
            pltpu.VMEM((own, width), bf16),
            pltpu.VMEM((3, 1, width), jnp.float32),
            pltpu.VMEM((2, head_size), jnp.float32),
            pltpu.VMEM((NZ, PARTS, NY, own, width // PARTS), bf16),
            pltpu.VMEM((width, 3 * head_size), bf16),
            pltpu.VMEM((NY, head_size, cols), bf16),
            pltpu.VMEM((2, clip, head_size), bf16),
            pltpu.VMEM((clip, head_size), bf16),
            pltpu.VMEM((clip, head_size), bf16),
            pltpu.VMEM((NZ, block, head_size), bf16),
            pltpu.VMEM((NZ, NY, block, head_size), bf16),
            pltpu.VMEM((2, NY, 4, own, cols), bf16),
            pltpu.VMEM((2, NY, 4, own, cols), bf16),
            pltpu.VMEM((NY, own, cols), bf16),
            pltpu.VMEM((NY, own, cols), bf16),
            dma((8,)),
            dma((NY, PARTS)),
            dma((NY, PARTS)),
            dma((NY,)),
            dma((NY,)),
            dma((NY,)),
            dma((NY,)),
            dma((2, 4, NY, PARTS)),
            dma((2, 4, NY, PARTS)),
            dma((NZ, NY)),
            dma((NZ, NY)),
            dma((2, NY, 4)),
            dma((2, NY, 4)),
            dma((NY,)),
            dma((NY,)),
        ],
        compiler_params=pltpu.CompilerParams(
            collective_id=0, has_side_effects=True, vmem_limit_bytes=48 << 20
        ),
    )(
        *[
            pltpu.with_memory_space_constraint(operand, pltpu.HBM)
            for operand in (
                hidden[0],
                jnp.transpose(modulation, (1, 0, 2)),
                jnp.transpose(w_qkv[0], (1, 0, 2)),
                qk_gain[0],
                w_out[0],
                stale_kv[0],
            )
        ],
        patch_start,
    )
    return received[None]


def solution(mesh):
    in_specs = (
        P("section", "seq", None),
        P("section", None, None),
        P("section", None, None, "seq"),
        P("section", None, None),
        P("section", "seq", None),
        P("section", None, None, "seq"),
        P("section"),
    )
    out_specs = P("section", "seq", None)
    return jax.shard_map(
        functools.partial(per_device, mesh.shape["section"]),
        mesh=mesh,
        in_specs=in_specs,
        out_specs=out_specs,
        check_vma=False,
    )
```

```python
import functools
import math

import jax
import jax.numpy as jnp
from jax import lax
from jax.experimental import pallas as pl
from jax.experimental.pallas import tpu as pltpu
from jax.sharding import PartitionSpec as P

MESH = pl.DeviceIdType.MESH
NY = 4
NZ = 8
PEERS = (1, 3, 2)
ORDER = (4, 3, -3, 2, -2, 1, -1, 0)
PARTS = 2
ARRIVALS = (
    (1, 0, 0, 0), (0, 0, 1, 0), (0, 0, 1, 1), (3, 0, 0, 0), (0, 1, 1, 0), (0, 1, 1, 1),
    (2, 0, 0, 0), (1, 0, 1, 0), (1, 0, 1, 1), (1, 1, 0, 0), (0, 0, 2, 0), (0, 0, 2, 1),
    (3, 1, 0, 0), (3, 0, 1, 0), (3, 0, 1, 1), (0, 1, 2, 0), (0, 1, 2, 1), (2, 1, 0, 0),
    (2, 0, 1, 0), (1, 0, 2, 0), (2, 0, 1, 1), (1, 0, 2, 1), (1, 1, 1, 0), (1, 1, 1, 1),
    (0, 0, 3, 0), (0, 0, 3, 1), (3, 1, 1, 0), (3, 1, 1, 1), (3, 0, 2, 0), (3, 0, 2, 1),
    (0, 1, 3, 0), (0, 1, 3, 1), (2, 1, 1, 0), (2, 1, 1, 1), (1, 0, 3, 0), (1, 0, 3, 1),
    (2, 0, 2, 0), (2, 0, 2, 1), (1, 1, 2, 0), (1, 1, 2, 1), (0, 0, 4, 0), (3, 1, 2, 1),
    (3, 0, 3, 1), (3, 1, 2, 0), (3, 0, 3, 0), (2, 1, 2, 1), (0, 1, 4, 0), (1, 0, 4, 1),
    (2, 0, 3, 1), (2, 1, 2, 0), (1, 1, 3, 1), (2, 0, 3, 0), (1, 1, 3, 0), (3, 1, 3, 1),
    (3, 0, 4, 1), (3, 1, 3, 0), (2, 1, 3, 0), (2, 1, 3, 1), (1, 1, 4, 1), (2, 0, 4, 0),
    (3, 1, 4, 1), (2, 1, 4, 0),
)


def kernel(
    sections,
    hid_hbm,
    mod_hbm,
    wq_hbm,
    gain_hbm,
    wo_hbm,
    st_hbm,
    start,
    out,
    hid,
    mod,
    gain,
    rows_all,
    w_all,
    w_cols,
    stale,
    keys,
    vals,
    queries,
    heads,
    part_out,
    part_in,
    hid_cols,
    out_rows,
    local_sem,
    y_send,
    y_recv,
    hid_send,
    hid_recv,
    w_send,
    w_recv,
    z_send,
    z_recv,
    head_send,
    head_recv,
    ring_send,
    ring_recv,
    out_send,
    out_recv,
):
    own, width = hid.shape
    head_size = gain.shape[1]
    block = NY * own
    cols = width // NY
    patch = block * NZ
    section = lax.axis_index("section")
    place = lax.axis_index("seq")
    y = place // NZ
    z = place % NZ
    after = (section + 1) % sections
    before = (section + sections - 1) % sections

    y_near = [(y + distance) % NY for distance in range(NY)]
    z_near = [(z + distance) % NZ for distance in range(NZ)]

    def y_at(distance):
        return y_near[distance % NY]

    def z_at(distance):
        return z_near[distance % NZ]

    def remote(src, dst, send, recv, yy, zz, sec=section):
        return pltpu.make_async_remote_copy(
            src_ref=src,
            dst_ref=dst,
            send_sem=send,
            recv_sem=recv,
            device_id=(sec, yy * NZ + zz),
            device_id_type=MESH,
        )

    first_local = [
        pltpu.make_async_copy(src, dst, local_sem.at[5 + j])
        for j, (src, dst) in enumerate(
            ((hid_hbm, hid), (mod_hbm, mod), (gain_hbm, gain))
        )
    ]
    for copy in first_local:
        copy.start()
    local = [
        pltpu.make_async_copy(
            wq_hbm.at[j], w_all.at[:, pl.ds(j * head_size, head_size)], local_sem.at[j]
        )
        for j in range(3)
    ]
    local.append(pltpu.make_async_copy(st_hbm, stale, local_sem.at[3]))
    my_cols = pl.ds(pl.multiple_of(y * cols, cols), cols)
    local.append(
        pltpu.make_async_copy(wo_hbm.at[:, my_cols], w_cols.at[y], local_sem.at[4])
    )
    for copy in local:
        copy.start()

    barrier = pltpu.get_barrier_semaphore()
    partners = [(section, y_at(e) * NZ + z) for e in PEERS]
    partners += [(section, y * NZ + z_at(s)) for s in (1, -1, 2, -2)]
    partners += [(after, yy * NZ + z) for yy in range(NY)]
    partners += [(before, yy * NZ + z) for yy in range(NY)]
    for partner in partners:
        pl.semaphore_signal(barrier, inc=1, device_id=partner, device_id_type=MESH)

    for copy in first_local:
        copy.wait()
    values = hid[...].astype(jnp.float32)
    average = jnp.mean(values, axis=-1, keepdims=True)
    centred = values - average
    spread = jnp.mean(centred * centred, axis=-1, keepdims=True)
    scale = lax.rsqrt(spread + 1e-06)
    piece = width // PARTS

    def modulate(p):
        here = slice(p * piece, (p + 1) * piece)
        normed = centred[:, here] * scale
        mixed = normed * (1.0 + mod[1, :, here]) + mod[0, :, here]
        rows_all[z, p, y] = mixed.astype(jnp.bfloat16)

    modulate(0)
    pl.semaphore_wait(barrier, len(partners))

    def y_copy(e, p):
        mine = rows_all.at[z, p, y]
        return remote(mine, mine, y_send.at[e, p], y_recv.at[e, p], y_at(e), z)

    def y_wait(e, p):
        slot = rows_all.at[z, p, y_at(-e)]
        remote(slot, slot, y_send.at[e, p], y_recv.at[e, p], y_at(e), z).wait_recv()

    def z_copy(way, h, e, p):
        s = 1 - 2 * way
        slot = rows_all.at[z_at(-s * h), p, y_at(-e)]
        sems = (z_send.at[way, h, e, p], z_recv.at[way, h, e, p])
        return remote(slot, slot, *sems, y, z_at(s))

    def z_wait(way, h, e, p):
        s = 1 - 2 * way
        slot = rows_all.at[z_at(-s * (h + 1)), p, y_at(-e)]
        sems = (z_send.at[way, h, e, p], z_recv.at[way, h, e, p])
        remote(slot, slot, *sems, y, z_at(s)).wait_recv()

    def reach(way, e):
        return 4 if (e % 2) == way else 3

    def hid_copy(e):
        there = pl.ds(pl.multiple_of(y_at(e) * cols, cols), cols)
        return remote(
            hid.at[:, there], hid_cols.at[y], hid_send.at[e], hid_recv.at[e], y_at(e), z
        )

    def w_copy(e):
        there = pl.ds(pl.multiple_of(y_at(e) * cols, cols), cols)
        return remote(
            wo_hbm.at[:, there], w_cols.at[y], w_send.at[e], w_recv.at[e], y_at(e), z
        )

    for p in range(PARTS):
        if p:
            modulate(p)
        for way in range(2):
            z_copy(way, 0, 0, p).start()
        if p == 0:
            for e in PEERS:
                y_copy(e, p).start()
    hid_cols[y] = hid[:, my_cols]

    local[3].wait()
    first = start[0]
    row = lax.broadcasted_iota(jnp.int32, (patch, head_size), 0)
    for j, target in ((0, keys), (1, vals)):
        low = stale[j, pl.ds(0, patch), :].astype(jnp.float32)
        high = stale[j, pl.ds(patch, patch), :].astype(jnp.float32)
        target[pl.ds(0, patch), :] = jnp.where(row < first, low, high).astype(
            jnp.bfloat16
        )
    query_scale = math.log2(math.e) / math.sqrt(head_size)

    def product(places, p):
        rows = [rows_all[at, p].reshape(block, piece) for at in places]
        return jnp.dot(
            rows[0] if len(rows) == 1 else jnp.concatenate(rows, axis=0),
            w_all[p * piece : (p + 1) * piece, :],
            preferred_element_type=jnp.float32,
        )

    def project(places, merged=None):
        if merged is None:
            merged = product(places, 0)
        merged += product(places, 1)
        q = merged[:, :head_size]
        k = merged[:, head_size : 2 * head_size]
        v = merged[:, 2 * head_size :].astype(jnp.bfloat16)
        q = q * lax.rsqrt(jnp.mean(q * q, axis=-1, keepdims=True) + 1e-06)
        q = (q * (gain[0:1, :] * query_scale)).astype(jnp.bfloat16)
        k = k * lax.rsqrt(jnp.mean(k * k, axis=-1, keepdims=True) + 1e-06)
        k = (k * gain[1:2, :]).astype(jnp.bfloat16)
        for i, at in enumerate(places):
            here = slice(i * block, (i + 1) * block)
            there = pl.ds(pl.multiple_of(patch + at * block, block), block)
            queries[at] = q[here]
            keys[there, :] = k[here]
            vals[there, :] = v[here]

    left = [sum(hops == h for _, _, hops, _ in ARRIVALS) for h in range(5)]
    last_firsts = sum((p, hops) == (0, 4) for _, p, hops, _ in ARRIVALS)
    for e, p, h, way in ARRIVALS:
        if h == 0:
            y_wait(e, p)
            for onward in range(2):
                z_copy(onward, 0, e, p).start()
            if p == 0:
                y_copy(e, 0).wait_send()
                y_copy(e, 1).start()
        else:
            z_wait(way, h - 1, e, p)
            if h < reach(way, e):
                z_copy(way, h, e, p).start()
        left[h] -= 1
        if h == 4 and p == 0:
            last_firsts -= 1
            if not last_firsts:
                early = product([z_at(4)], 0)
        if left[h]:
            continue
        if h == 0:
            for peer in PEERS:
                w_copy(peer).start()
            for peer in PEERS:
                hid_copy(peer).start()
        elif h == 4:
            project([z_at(4)], early)
        elif h == 1:
            for j in range(3):
                local[j].wait()
            project([z, z_at(-h), z_at(h)])
        else:
            project([z_at(-h), z_at(h)])

    def head_copy(i, e):
        mine = heads.at[z_at(ORDER[i]), y]
        return remote(mine, mine, head_send.at[i, e], head_recv.at[i, e], y_at(e), z)

    def attend(i):
        at = z_at(ORDER[i])
        scores = lax.dot_general(
            queries[at],
            keys[...],
            (((1,), (1,)), ((), ())),
            preferred_element_type=jnp.float32,
        )
        highest = jnp.max(scores, axis=-1, keepdims=True)
        raised = jnp.exp2(scores - highest)
        total = jnp.sum(raised, axis=-1, keepdims=True)
        mixed_values = jnp.dot(
            raised.astype(jnp.bfloat16), vals[...], preferred_element_type=jnp.float32
        )
        heads[at, y] = (mixed_values / total).astype(jnp.bfloat16)
        for e in PEERS:
            head_copy(i, e).start()

    def ring_copy(way, part, k):
        return remote(
            part_out.at[way, part, k - 1],
            part_in.at[way, part, k - 1],
            ring_send.at[way, part, k - 1],
            ring_recv.at[way, part, k - 1],
            y,
            z_at((1 - 2 * way) * (2 if k == 4 else 1)),
        )

    def length(way, part):
        return 4 if way == part % 2 else 3

    def out_copy(yy):
        return remote(
            out_rows.at[yy],
            out.at[:, my_cols],
            out_send.at[yy],
            out_recv.at[y],
            yy,
            z,
            after,
        )

    gate = mod[2, :, my_cols]

    def layer_rows(part, total):
        for way in range(2):
            ring_copy(way, part, 1).wait_recv()
            total += part_in[way, part, 0].astype(jnp.float32)
        layer_out = hid_cols[part].astype(jnp.float32) + gate * total
        out_rows[part] = layer_out.astype(jnp.bfloat16)
        out_copy(part).start()

    def finish(i):
        offset = ORDER[i]
        at = z_at(offset)
        for e in PEERS:
            slot = heads.at[at, y_at(-e)]
            remote(
                slot, slot, head_send.at[i, e], head_recv.at[i, e], y_at(e), z
            ).wait_recv()
        four = jnp.concatenate([heads[at, yy] for yy in range(NY)], axis=1)
        summed = jnp.dot(
            four,
            w_cols[...].reshape(NY * head_size, cols),
            preferred_element_type=jnp.float32,
        )
        pieces = [summed[part * own : (part + 1) * own] for part in range(NY)]
        k = abs(offset)
        if k == 0:
            for part in range(NY):
                layer_rows(part, pieces[part])
            return
        ways = (0, 1) if k == 4 else ((0,) if offset > 0 else (1,))
        for way in ways:
            for part in range(NY):
                if k > length(way, part):
                    continue
                added = pieces[part]
                came = [k + 1] if k < 3 else []
                if k == 2 and length(way, part) == 4:
                    came.append(4)
                for c in came:
                    ring_copy(way, part, c).wait_recv()
                    added += part_in[way, part, c - 1].astype(jnp.float32)
                part_out[way, part, k - 1] = added.astype(jnp.bfloat16)
                ring_copy(way, part, k).start()

    blocks = len(ORDER)
    ahead = 3
    for i in range(blocks + ahead):
        if i < blocks:
            attend(i)
        if i == ahead:
            for e in PEERS:
                slot = w_cols.at[y_at(-e)]
                remote(slot, slot, w_send.at[e], w_recv.at[e], y_at(e), z).wait_recv()
                slot = hid_cols.at[y_at(-e)]
                remote(
                    slot, slot, hid_send.at[e], hid_recv.at[e], y_at(e), z
                ).wait_recv()
            local[4].wait()
        if i >= ahead:
            finish(i - ahead)

    for e in PEERS:
        y_copy(e, 1).wait_send()
        hid_copy(e).wait_send()
        w_copy(e).wait_send()
    for e in range(NY):
        for way in range(2):
            for h in range(reach(way, e)):
                for p in range(PARTS):
                    z_copy(way, h, e, p).wait_send()
    for i in range(blocks):
        for e in PEERS:
            head_copy(i, e).wait_send()
    for way in range(2):
        for part in range(NY):
            for k in range(1, length(way, part) + 1):
                ring_copy(way, part, k).wait_send()
    for yy in range(NY):
        out_copy(yy).wait_send()
    for yy in range(NY):
        slot = out.at[:, pl.ds(yy * cols, cols)]
        remote(
            out_rows.at[yy], slot, out_send.at[yy], out_recv.at[yy], yy, z, after
        ).wait_recv()


def per_device(sections, hidden, modulation, w_qkv, qk_gain, w_out, stale_kv, patch_start):
    own, width = hidden.shape[1:]
    head_size = qk_gain.shape[2]
    clip = stale_kv.shape[2]
    block = NY * own
    cols = width // NY
    bf16 = jnp.bfloat16
    dma = pltpu.SemaphoreType.DMA
    hbm = pl.BlockSpec(memory_space=pltpu.HBM)
    vmem = pl.BlockSpec(memory_space=pltpu.VMEM)
    smem = pl.BlockSpec(memory_space=pltpu.SMEM)
    received = pl.pallas_call(
        functools.partial(kernel, sections),
        out_shape=jax.ShapeDtypeStruct((own, width), bf16),
        in_specs=[hbm] * 6 + [smem],
        out_specs=vmem,
        scratch_shapes=[
            pltpu.VMEM((own, width), bf16),
            pltpu.VMEM((3, 1, width), jnp.float32),
            pltpu.VMEM((2, head_size), jnp.float32),
            pltpu.VMEM((NZ, PARTS, NY, own, width // PARTS), bf16),
            pltpu.VMEM((width, 3 * head_size), bf16),
            pltpu.VMEM((NY, head_size, cols), bf16),
            pltpu.VMEM((2, clip, head_size), bf16),
            pltpu.VMEM((clip, head_size), bf16),
            pltpu.VMEM((clip, head_size), bf16),
            pltpu.VMEM((NZ, block, head_size), bf16),
            pltpu.VMEM((NZ, NY, block, head_size), bf16),
            pltpu.VMEM((2, NY, 4, own, cols), bf16),
            pltpu.VMEM((2, NY, 4, own, cols), bf16),
            pltpu.VMEM((NY, own, cols), bf16),
            pltpu.VMEM((NY, own, cols), bf16),
            dma((8,)),
            dma((NY, PARTS)),
            dma((NY, PARTS)),
            dma((NY,)),
            dma((NY,)),
            dma((NY,)),
            dma((NY,)),
            dma((2, 4, NY, PARTS)),
            dma((2, 4, NY, PARTS)),
            dma((NZ, NY)),
            dma((NZ, NY)),
            dma((2, NY, 4)),
            dma((2, NY, 4)),
            dma((NY,)),
            dma((NY,)),
        ],
        compiler_params=pltpu.CompilerParams(
            collective_id=0, has_side_effects=True, vmem_limit_bytes=48 << 20
        ),
    )(
        *[
            pltpu.with_memory_space_constraint(operand, pltpu.HBM)
            for operand in (
                hidden[0],
                jnp.transpose(modulation, (1, 0, 2)),
                jnp.transpose(w_qkv[0], (1, 0, 2)),
                qk_gain[0],
                w_out[0],
                stale_kv[0],
            )
        ],
        patch_start,
    )
    return received[None]


def solution(mesh):
    in_specs = (
        P("section", "seq", None),
        P("section", None, None),
        P("section", None, None, "seq"),
        P("section", None, None),
        P("section", "seq", None),
        P("section", None, None, "seq"),
        P("section"),
    )
    out_specs = P("section", "seq", None)
    return jax.shard_map(
        functools.partial(per_device, mesh.shape["section"]),
        mesh=mesh,
        in_specs=in_specs,
        out_specs=out_specs,
        check_vma=False,
    )
```
